32 devices in a mesh: dp: 8 (over z, y), tensor: 4 (over x, core).
Axes of the slice: x: 2, y: 2, z: 4, core: 2. Of those that a mesh axis runs over, the one named last changes fastest.
Arguments:
- hidden: bfloat16 [1024, 7168], P('dp', 'tensor'), may hold values from -6 to 6
- hash_rows: int32 [1024, 4], P('dp', 'tensor'), may hold values from 0 to 8191, as said below
- memory_table: bfloat16 [8192, 896], P(('dp', 'tensor')), may hold values from -6 to 6
- key_weight: bfloat16 [3584, 7168], P(None, 'tensor'), may hold values from -0.09375 to 0.09375
- value_weight: bfloat16 [3584, 7168], P(None, 'tensor'), may hold values from -0.09375 to 0.09375
- hidden_gain: float32 [7168], P('tensor'), may hold values from 0.1 to 1.9
- key_gain: float32 [7168], P('tensor'), may hold values from 0.1 to 1.9
Outputs:
- joined: bfloat16 [1024, 7168], P('dp', 'tensor')
The draws below stay inside these ranges and needn't reach their ends.
Inputs may be any that keep to these rules, and one draw needn't show every extreme that they name: `hash_rows`: row r lies in the block of 256 rows held by device r // 256 of dp+tensor. Of the lookups that one device holds (128 requests of its dp group times its 4 / 4 heads), at most 8 fall into any one device's block, and in every draw some device's block receives exactly 8 from every device.
All inputs are finite; a program needn't handle non-finite values.
Results may differ from the reference program's by a relative error of at most 0.0014.
Values may be sent and summed in bfloat16 or wider, within the bound.
A program may use at most 64 MiB of HBM per device.

```python
import jax
import jax.numpy as jnp
from jax import lax

D = 7168
HEADW = 896
HEADS = 4
REQ = 128
ROWS_DEV = 256
MEM = 3584
TOKENS = 1024
ROWS = 8192
CAP = 8
N_DP = 8
N_TENSOR = 4


def draw_hash_rows(key, part):
    owners = N_DP * N_TENSOR
    per_device = REQ * (HEADS // N_TENSOR)
    slot_count = owners * CAP
    hot_owner = jax.random.randint(jax.random.fold_in(key, 11), (), 0, owners)
    slot_owner = jnp.arange(slot_count, dtype=jnp.int32) // CAP
    slot_rank = jnp.arange(slot_count, dtype=jnp.int32) % CAP

    def one_device(device_index):
        device_key = jax.random.fold_in(jax.random.fold_in(key, 23), device_index)
        shuffle_order = jax.random.permutation(jax.random.fold_in(device_key, 1), slot_count)
        placing = jnp.zeros((slot_count,), jnp.int32).at[shuffle_order].set(jnp.arange(slot_count, dtype=jnp.int32))
        priority = jnp.where(slot_owner == hot_owner, slot_rank - CAP, placing)
        chosen = jnp.argsort(priority, stable=True)[:per_device]
        picked = slot_owner[chosen]
        shuffled = picked[jax.random.permutation(jax.random.fold_in(device_key, 2), per_device)]
        local_rows = jax.random.randint(jax.random.fold_in(device_key, 3), (per_device,), 0, ROWS_DEV)
        return shuffled * ROWS_DEV + local_rows
    drawn = jax.vmap(one_device)(jnp.arange(owners, dtype=jnp.int32))
    blocks = drawn.reshape(N_DP, N_TENSOR, REQ, HEADS // N_TENSOR)
    return jnp.transpose(blocks, (0, 2, 1, 3)).reshape(N_DP * REQ, HEADS).astype(jnp.int32)


def block_levels(rng, dims, split, least, largest):
    loudness, own = 1.0, jax.random.fold_in(rng, 6)
    for dim, blocks in split:
        draws = jnp.exp(jax.random.uniform(jax.random.fold_in(own, dim), (blocks,), jnp.float32, least / len(split), largest / len(split)))
        loudness = loudness * jnp.repeat(draws, dims[dim] // blocks).reshape([-1 if axis == dim else 1 for axis in range(len(dims))])
    return loudness


def gaussian(stream_key, extent, scale, bound, cuts=(), kind=jnp.bfloat16):
    entries = jax.random.normal(stream_key, extent, jnp.float32) * scale
    if len(cuts) > 0:
        entries = block_levels(stream_key, extent, cuts, -0.22, 0.18) * entries
    return jnp.clip(entries, min=-bound, max=bound).astype(kind)


def setup_inputs(seed: int = 0) -> dict:
    key_of = jax.random.split(jax.random.key(seed), 8)
    hidden = gaussian(key_of[0], (TOKENS, D), 1.0, 6.0, ((0, 8), (1, 4)))
    hash_rows = draw_hash_rows(jax.random.fold_in(key_of[7], 71), 0)
    memory_table = gaussian(key_of[2], (ROWS, HEADW), 1.0, 6.0, ((0, 32),))
    key_weight = gaussian(key_of[3], (MEM, D), MEM ** -0.5, 0.09375, ((1, 4),))
    value_weight = gaussian(key_of[4], (MEM, D), MEM ** -0.5, 0.09375, ((1, 4),))
    hidden_gain = jnp.clip(1.0 + 0.18 * jax.random.normal(key_of[5], (D,), jnp.float32), 0.1, 1.9)
    key_gain = jnp.clip(1.0 + 0.18 * jax.random.normal(key_of[6], (D,), jnp.float32), 0.1, 1.9)
    return {"hidden": hidden, "hash_rows": hash_rows, "memory_table": memory_table, "key_weight": key_weight, "value_weight": value_weight, "hidden_gain": hidden_gain, "key_gain": key_gain}


epsilon = 1e-06

def reference(hidden, hash_rows, memory_table, key_weight, value_weight, hidden_gain, key_gain):

    def group_output(arrays):
        hidden_rows, index_rows = arrays
        memory = memory_table[index_rows].reshape(index_rows.shape[0], MEM)
        key = jnp.dot(memory, key_weight, preferred_element_type=jnp.float32)
        projected = jnp.dot(memory, value_weight, preferred_element_type=jnp.float32)
        hidden_float = hidden_rows.astype(jnp.float32)
        hidden_power = lax.optimization_barrier(jnp.mean(hidden_float * hidden_float, axis=1))
        key_power = lax.optimization_barrier(jnp.mean(key * key, axis=1))
        crossing = lax.optimization_barrier(jnp.sum(hidden_float * hidden_gain * key * key_gain, axis=1))
        agreement = crossing * lax.rsqrt(hidden_power + epsilon) * lax.rsqrt(key_power + epsilon)
        gate_value = jax.nn.sigmoid(agreement / jnp.sqrt(jnp.float32(D)))
        return (hidden_float + gate_value[:, None] * projected).astype(jnp.bfloat16)
    outputs = lax.map(group_output, (hidden.reshape(N_DP, REQ, D), hash_rows.reshape(N_DP, REQ, HEADS)))
    return outputs.reshape(N_DP * REQ, D)
```

```python
import functools
import math

import jax
import jax.numpy as jnp
from jax import lax
from jax.experimental import pallas as pl
from jax.experimental.pallas import tpu as pltpu
from jax.sharding import PartitionSpec as P

MESH = pl.DeviceIdType.MESH
epsilon = 1e-06
F32, BF16 = jnp.float32, jnp.bfloat16


def dot(a, b):
    return jnp.dot(a, b, preferred_element_type=F32)


def kernel(groups, heads, slots, ids_ref, hg_ref, kg_ref, table_hbm, hidden_hbm, wk_hbm, wv_hbm, out_ref,
           ids, table, hidden, wk, wv, sending, rows, place, mem, acc_k, acc_v, stats,
           local_sem, w_sem, own_sem, id_send, id_recv, list_send, list_recv,
           row_send, row_recv, pass_send, pass_recv, stat_send, stat_recv):
    me_p, me_t = lax.axis_index("dp"), lax.axis_index("tensor")
    held, width = table.shape
    requests, columns = hidden.shape
    model = columns * heads
    chunk = 256 if columns % 256 == 0 else 128

    def here(source, target, sem):
        return pltpu.make_async_copy(source, target, sem)

    def there(source, target, send, recv, p, t):
        return pltpu.make_async_remote_copy(
            src_ref=source, dst_ref=target, send_sem=send, recv_sem=recv,
            device_id={"dp": p, "tensor": t}, device_id_type=MESH)

    def ahead(i):
        return lax.rem(me_p + i, groups)

    def behind(i):
        return lax.rem(me_p + groups - i, groups)

    own_ids = here(ids_ref.at[0], ids.at[me_p, me_t], local_sem.at[0])
    own_ids.start()
    table_copy = here(table_hbm, table, local_sem.at[1])
    table_copy.start()
    weights = []
    for h in range(heads):
        for which, (source, target) in enumerate(((wk_hbm, wk), (wv_hbm, wv))):
            copy = here(source.at[pl.ds(h * width, width), :], target.at[h], w_sem.at[h, which])
            copy.start()
            weights.append(copy)
    hidden_copy = here(hidden_hbm, hidden, local_sem.at[2])
    hidden_copy.start()

    barrier = pltpu.get_barrier_semaphore()

    @pl.loop(1, groups)
    def _(i):
        pl.semaphore_signal(barrier, inc=1, device_id={"dp": ahead(i), "tensor": me_t}, device_id_type=MESH)

    for m in range(1, heads):
        pl.semaphore_signal(barrier, inc=1, device_id={"dp": me_p, "tensor": me_t ^ m}, device_id_type=MESH)
    pl.semaphore_wait(barrier, groups - 1 + heads - 1)

    def id_copy(m, t):
        return there(ids_ref.at[0], ids.at[me_p, t], id_send.at[m - 1], id_recv.at[m - 1], me_p, me_t ^ m)

    for m in range(1, heads):
        id_copy(m, me_t).start()
    own_ids.wait()
    for m in range(1, heads):
        id_copy(m, me_t ^ m).wait_recv()

    def list_copy(i, p):
        return there(ids.at[me_p], ids.at[p], list_send.at[i - 1], list_recv.at[i - 1], ahead(i), me_t)

    @pl.loop(1, groups)
    def _(i):
        list_copy(i, me_p).start()

    sub = lax.broadcasted_iota(jnp.int32, (requests, requests), 0)
    lane = lax.broadcasted_iota(jnp.int32, (requests, requests), 1)
    spots = lax.broadcasted_iota(jnp.int32, (requests, groups * heads * slots), 1).astype(F32)
    for h in range(heads):
        numbers = ids[me_p, h].astype(F32)
        owner = jnp.broadcast_to(jnp.floor((numbers + 0.5) * (1.0 / held)), (requests, requests))
        column = jnp.sum(jnp.where(sub == lane, owner, 0.0), axis=1, keepdims=True)
        rank = jnp.sum(jnp.where((owner == column) & (lane < sub), 1.0, 0.0), axis=1, keepdims=True)
        owner_p = jnp.floor((column + 0.5) * (1.0 / heads))
        owner_t = column - owner_p * heads
        spot = (owner_t * groups + owner_p) * slots + rank
        place[h] = jnp.where(spots == spot, 1.0, 0.0).astype(BF16)

    hidden_copy.wait()
    hidden_squares = jnp.zeros((requests, 1), F32)
    for c in range(columns // chunk):
        part = hidden[:, c * chunk:(c + 1) * chunk].astype(F32)
        hidden_squares += jnp.sum(part * part, axis=1, keepdims=True)

    @pl.loop(1, groups)
    def _(i):
        list_copy(i, behind(i)).wait_recv()

    lists = jnp.concatenate([ids[:, h].reshape(groups, requests) for h in range(heads)], axis=0)
    first = (me_p * heads + me_t) * held
    mine = (lists >= first) & (lists < first + held)
    earlier = jnp.where(sub < lane, 1.0, 0.0).astype(BF16)
    order = dot(jnp.where(mine, 1.0, 0.0).astype(BF16), earlier)
    order = jnp.where(mine, order, -1.0).astype(BF16)
    local = jnp.where(mine, lists - first, 0).astype(F32).astype(BF16)
    total = heads * groups * slots
    row = lax.broadcasted_iota(jnp.int32, (total, heads * groups), 0)
    source = lax.broadcasted_iota(jnp.int32, (total, heads * groups), 1) * slots
    spread = jnp.where((row >= source) & (row < source + slots), 1.0, 0.0).astype(BF16)
    slot = (lax.broadcasted_iota(jnp.int32, (total, requests), 0) & (slots - 1)).astype(F32)
    wanted = jnp.sum(jnp.where(dot(spread, order) == slot, dot(spread, local), 0.0), axis=1, keepdims=True)
    choose = jnp.where(
        lax.broadcasted_iota(jnp.int32, (total, held), 1).astype(F32) == wanted, 1.0, 0.0).astype(BF16)
    table_copy.wait()

    def row_copy(h, i, p):
        return there(sending.at[h, ahead(i)], rows.at[h, me_t, p],
                     row_send.at[h, i - 1], row_recv.at[h, i - 1], ahead(i), me_t)

    per_head = groups * slots
    for h in range(heads):
        block = dot(choose[h * per_head:(h + 1) * per_head], table[...])
        sending[h] = block.reshape(groups, slots, width).astype(BF16)

        @pl.loop(1, groups)
        def _(i):
            row_copy(h, i, me_p).start()

        here(sending.at[h, me_p], rows.at[h, me_t, me_p], own_sem.at[h]).start()

    def pass_on(h, bit, m, t):
        return there(rows.at[h, me_t ^ m], rows.at[h, t], pass_send.at[h, (m | bit) - 1],
                     pass_recv.at[h, (m | bit) - 1], me_p, me_t ^ bit)

    bits, bit = [], heads // 2
    while bit:
        bits.append(bit)
        bit //= 2

    def begin(h):
        here(sending.at[h, me_p], rows.at[h, me_t, me_p], own_sem.at[h]).wait()

        @pl.loop(1, groups)
        def _(i):
            row_copy(h, i, behind(i)).wait_recv()

        for b in bits:
            pass_on(h, b, 0, me_t).start()

    def onward(h):
        masks = [0]
        for n, b in enumerate(bits):
            if n:
                for m in masks[1:]:
                    pass_on(h, b, m, me_t ^ m).start()
            if n < len(bits) - 1:
                for m in masks:
                    pass_on(h, b, m, me_t ^ m ^ b).wait_recv()
            masks = masks + [m | b for m in masks]

    def finish(h):
        b = bits[-1]
        for m in range(0, heads, 2):
            pass_on(h, b, m, me_t ^ m ^ b).wait_recv()

    def multiply(h):
        finish(h)
        mem[...] = dot(place[h], rows[h].reshape(groups * heads * slots, width)).astype(BF16)
        weights[2 * h].wait()
        weights[2 * h + 1].wait()

        @pl.loop(0, columns // chunk)
        def _(c):
            part = pl.ds(pl.multiple_of(c * chunk, chunk), chunk)
            for w, acc in ((wk, acc_k), (wv, acc_v)):
                value = dot(mem[...], w[h, :, part])
                acc[:, part] = value if h == 0 else acc[:, part] + value

    for h in range(heads):
        begin(h)
        if h:
            multiply(h - 1)
        onward(h)
    multiply(heads - 1)

    key_squares = jnp.zeros((requests, 1), F32)
    crossing = jnp.zeros((requests, 1), F32)
    for c in range(columns // chunk):
        part = slice(c * chunk, (c + 1) * chunk)
        key = acc_k[:, part]
        key_squares += jnp.sum(key * key, axis=1, keepdims=True)
        scaled = hidden[:, part].astype(F32) * hg_ref[:, part] * (key * kg_ref[:, part])
        crossing += jnp.sum(scaled, axis=1, keepdims=True)
    lanes = lax.broadcasted_iota(jnp.int32, (requests, 128), 1)
    packed = jnp.where(lanes == 0, hidden_squares, jnp.where(lanes == 1, key_squares,
                       jnp.where(lanes == 2, crossing, 0.0)))
    stats[0] = packed.T[:8]

    def stat_copy(m):
        return there(stats.at[0], stats.at[m], stat_send.at[m - 1], stat_recv.at[m - 1], me_p, me_t ^ m)

    for m in range(1, heads):
        stat_copy(m).start()
    for m in range(1, heads):
        stat_copy(m).wait_recv()
    summed = stats[0]
    for m in range(1, heads):
        summed += stats[m]
    turned = jnp.concatenate([summed, jnp.zeros((120, requests), F32)], axis=0).T
    hidden_total, key_total, cross_total = turned[:, 0:1], turned[:, 1:2], turned[:, 2:3]
    agreement = (cross_total * lax.rsqrt(hidden_total / model + epsilon)
                 * lax.rsqrt(key_total / model + epsilon))
    gate = jax.nn.sigmoid(agreement / math.sqrt(model))
    for c in range(columns // chunk):
        part = slice(c * chunk, (c + 1) * chunk)
        out_ref[:, part] = (hidden[:, part].astype(F32) + gate * acc_v[:, part]).astype(BF16)

    for m in range(1, heads):
        id_copy(m, me_t).wait_send()
        stat_copy(m).wait_send()

    @pl.loop(1, groups)
    def _(i):
        list_copy(i, me_p).wait_send()
        for h in range(heads):
            row_copy(h, i, me_p).wait_send()

    for h in range(heads):
        masks = [0]
        for b in bits:
            for m in masks:
                pass_on(h, b, m, me_t ^ m).wait_send()
            masks = masks + [m | b for m in masks]


def local(groups, heads, hidden, hash_rows, memory_table, key_weight, value_weight, hidden_gain, key_gain):
    requests, columns = hidden.shape
    held, width = memory_table.shape
    assert hash_rows.shape[1] == 1 and heads & (heads - 1) == 0 and heads > 1
    slots = max(8, 2 * max(1, hash_rows.size // (groups * heads)))
    any_space = pl.BlockSpec(memory_space=pl.ANY)
    vmem = pl.BlockSpec(memory_space=pltpu.VMEM)
    dma = pltpu.SemaphoreType.DMA
    return pl.pallas_call(
        functools.partial(kernel, groups, heads, slots),
        out_shape=jax.ShapeDtypeStruct((requests, columns), BF16),
        in_specs=[vmem] * 3 + [any_space] * 4,
        out_specs=vmem,
        scratch_shapes=[
            pltpu.VMEM((groups, heads, 1, requests), jnp.int32),
            pltpu.VMEM((held, width), BF16),
            pltpu.VMEM((requests, columns), BF16),
            pltpu.VMEM((heads, width, columns), BF16),
            pltpu.VMEM((heads, width, columns), BF16),
            pltpu.VMEM((heads, groups, slots, width), BF16),
            pltpu.VMEM((heads, heads, groups, slots, width), BF16),
            pltpu.VMEM((heads, requests, groups * heads * slots), BF16),
            pltpu.VMEM((requests, width), BF16),
            pltpu.VMEM((requests, columns), F32),
            pltpu.VMEM((requests, columns), F32),
            pltpu.VMEM((heads, 8, requests), F32),
            dma((3,)), dma((heads, 2)), dma((heads,)),
            dma((heads - 1,)), dma((heads - 1,)),
            dma((groups - 1,)), dma((groups - 1,)),
            dma((heads, groups - 1)), dma((heads, groups - 1)),
            dma((heads, heads - 1)), dma((heads, heads - 1)),
            dma((heads - 1,)), dma((heads - 1,)),
        ],
        compiler_params=pltpu.CompilerParams(
            collective_id=0, has_side_effects=True, vmem_limit_bytes=60 * 1024 * 1024),
    )(hash_rows.reshape(1, 1, requests), hidden_gain.reshape(1, columns), key_gain.reshape(1, columns),
      memory_table, hidden, key_weight, value_weight)


def solution(mesh):
    return jax.shard_map(
        functools.partial(local, mesh.shape["dp"], mesh.shape["tensor"]),
        mesh=mesh,
        in_specs=(
            P("dp", "tensor"),
            P("dp", "tensor"),
            P(("dp", "tensor"), None),
            P(None, "tensor"),
            P(None, "tensor"),
            P("tensor"),
            P("tensor"),
        ),
        out_specs=P("dp", "tensor"),
        check_vma=False,
    )
```

```python
import functools
import math

import jax
import jax.numpy as jnp
from jax import lax
from jax.experimental import pallas as pl
from jax.experimental.pallas import tpu as pltpu
from jax.sharding import PartitionSpec as P

MESH = pl.DeviceIdType.MESH
epsilon = 1e-06
F32, BF16 = jnp.float32, jnp.bfloat16


def dot(a, b):
    return jnp.dot(a, b, preferred_element_type=F32)


def kernel(groups, heads, slots, ids_ref, hg_ref, kg_ref, table_hbm, hidden_hbm, wk_hbm, wv_hbm, out_ref,
           ids, table, hidden, wk, wv, sending, rows, place, mem, acc_k, acc_v, stats,
           local_sem, w_sem, own_sem, id_send, id_recv, list_send, list_recv,
           row_send, row_recv, pass_send, pass_recv, stat_send, stat_recv):
    me_p, me_t = lax.axis_index("dp"), lax.axis_index("tensor")
    held, width = table.shape
    requests, columns = hidden.shape
    model = columns * heads
    chunk = 256 if columns % 256 == 0 else 128

    def here(source, target, sem):
        return pltpu.make_async_copy(source, target, sem)

    def there(source, target, send, recv, p, t):
        return pltpu.make_async_remote_copy(
            src_ref=source, dst_ref=target, send_sem=send, recv_sem=recv,
            device_id={"dp": p, "tensor": t}, device_id_type=MESH)

    def ahead(i):
        return lax.rem(me_p + i, groups)

    def behind(i):
        return lax.rem(me_p + groups - i, groups)

    own_ids = here(ids_ref.at[0], ids.at[me_p, me_t], local_sem.at[0])
    own_ids.start()
    table_copy = here(table_hbm, table, local_sem.at[1])
    table_copy.start()
    weights = []
    for h in range(heads):
        for which, (source, target) in enumerate(((wk_hbm, wk), (wv_hbm, wv))):
            copy = here(source.at[pl.ds(h * width, width), :], target.at[h], w_sem.at[h, which])
            copy.start()
            weights.append(copy)
    hidden_copy = here(hidden_hbm, hidden, local_sem.at[2])
    hidden_copy.start()

    barrier = pltpu.get_barrier_semaphore()

    @pl.loop(1, groups)
    def _(i):
        pl.semaphore_signal(barrier, inc=1, device_id={"dp": ahead(i), "tensor": me_t}, device_id_type=MESH)

    for m in range(1, heads):
        pl.semaphore_signal(barrier, inc=1, device_id={"dp": me_p, "tensor": me_t ^ m}, device_id_type=MESH)
    pl.semaphore_wait(barrier, groups - 1 + heads - 1)

    def id_copy(m, t):
        return there(ids_ref.at[0], ids.at[me_p, t], id_send.at[m - 1], id_recv.at[m - 1], me_p, me_t ^ m)

    for m in range(1, heads):
        id_copy(m, me_t).start()
    own_ids.wait()
    for m in range(1, heads):
        id_copy(m, me_t ^ m).wait_recv()

    def list_copy(i, p):
        return there(ids.at[me_p], ids.at[p], list_send.at[i - 1], list_recv.at[i - 1], ahead(i), me_t)

    @pl.loop(1, groups)
    def _(i):
        list_copy(i, me_p).start()

    sub = lax.broadcasted_iota(jnp.int32, (requests, requests), 0)
    lane = lax.broadcasted_iota(jnp.int32, (requests, requests), 1)
    spots = lax.broadcasted_iota(jnp.int32, (requests, groups * heads * slots), 1).astype(F32)
    for h in range(heads):
        numbers = ids[me_p, h].astype(F32)
        owner = jnp.broadcast_to(jnp.floor((numbers + 0.5) * (1.0 / held)), (requests, requests))
        column = jnp.sum(jnp.where(sub == lane, owner, 0.0), axis=1, keepdims=True)
        rank = jnp.sum(jnp.where((owner == column) & (lane < sub), 1.0, 0.0), axis=1, keepdims=True)
        owner_p = jnp.floor((column + 0.5) * (1.0 / heads))
        owner_t = column - owner_p * heads
        spot = (owner_t * groups + owner_p) * slots + rank
        place[h] = jnp.where(spots == spot, 1.0, 0.0).astype(BF16)

    hidden_copy.wait()
    hidden_squares = jnp.zeros((requests, 1), F32)
    for c in range(columns // chunk):
        part = hidden[:, c * chunk:(c + 1) * chunk].astype(F32)
        hidden_squares += jnp.sum(part * part, axis=1, keepdims=True)

    @pl.loop(1, groups)
    def _(i):
        list_copy(i, behind(i)).wait_recv()

    lists = jnp.concatenate([ids[:, h].reshape(groups, requests) for h in range(heads)], axis=0)
    first = (me_p * heads + me_t) * held
    mine = (lists >= first) & (lists < first + held)
    earlier = jnp.where(sub < lane, 1.0, 0.0).astype(BF16)
    order = dot(jnp.where(mine, 1.0, 0.0).astype(BF16), earlier)
    order = jnp.where(mine, order, -1.0).astype(BF16)
    local = jnp.where(mine, lists - first, 0).astype(F32).astype(BF16)
    total = heads * groups * slots
    row = lax.broadcasted_iota(jnp.int32, (total, heads * groups), 0)
    source = lax.broadcasted_iota(jnp.int32, (total, heads * groups), 1) * slots
    spread = jnp.where((row >= source) & (row < source + slots), 1.0, 0.0).astype(BF16)
    slot = (lax.broadcasted_iota(jnp.int32, (total, requests), 0) & (slots - 1)).astype(F32)
    wanted = jnp.sum(jnp.where(dot(spread, order) == slot, dot(spread, local), 0.0), axis=1, keepdims=True)
    choose = jnp.where(
        lax.broadcasted_iota(jnp.int32, (total, held), 1).astype(F32) == wanted, 1.0, 0.0).astype(BF16)
    table_copy.wait()

    def row_copy(h, i, p):
        return there(sending.at[h, ahead(i)], rows.at[h, me_t, p],
                     row_send.at[h, i - 1], row_recv.at[h, i - 1], ahead(i), me_t)

    def send_rows(h):
        @pl.loop(1, groups)
        def _(i):
            row_copy(h, i, me_p).start()

    per_head = groups * slots
    for h in range(heads):
        block = dot(choose[h * per_head:(h + 1) * per_head], table[...])
        sending[h] = block.reshape(groups, slots, width).astype(BF16)
        here(sending.at[h, me_p], rows.at[h, me_t, me_p], own_sem.at[h]).start()
        if h < 2:
            send_rows(h)

    def pass_on(h, bit, m, t):
        return there(rows.at[h, me_t ^ m], rows.at[h, t], pass_send.at[h, (m | bit) - 1],
                     pass_recv.at[h, (m | bit) - 1], me_p, me_t ^ bit)

    bits, bit = [], heads // 2
    while bit:
        bits.append(bit)
        bit //= 2

    def begin(h):
        here(sending.at[h, me_p], rows.at[h, me_t, me_p], own_sem.at[h]).wait()

        @pl.loop(1, groups)
        def _(i):
            row_copy(h, i, behind(i)).wait_recv()

        for b in bits:
            pass_on(h, b, 0, me_t).start()
        if h + 2 < heads:
            send_rows(h + 2)

    def onward(h):
        masks = [0]
        for n, b in enumerate(bits):
            if n:
                for m in masks[1:]:
                    pass_on(h, b, m, me_t ^ m).start()
            if n < len(bits) - 1:
                for m in masks:
                    pass_on(h, b, m, me_t ^ m ^ b).wait_recv()
            masks = masks + [m | b for m in masks]

    def finish(h):
        b = bits[-1]
        for m in range(0, heads, 2):
            pass_on(h, b, m, me_t ^ m ^ b).wait_recv()

    def multiply(h):
        finish(h)
        mem[...] = dot(place[h], rows[h].reshape(groups * heads * slots, width)).astype(BF16)
        weights[2 * h].wait()
        weights[2 * h + 1].wait()

        @pl.loop(0, columns // chunk)
        def _(c):
            part = pl.ds(pl.multiple_of(c * chunk, chunk), chunk)
            for w, acc in ((wk, acc_k), (wv, acc_v)):
                value = dot(mem[...], w[h, :, part])
                acc[:, part] = value if h == 0 else acc[:, part] + value

    for step in range(heads + 2):
        if step < heads:
            begin(step)
        if step > 1:
            multiply(step - 2)
        if 0 < step <= heads:
            onward(step - 1)

    key_squares = jnp.zeros((requests, 1), F32)
    crossing = jnp.zeros((requests, 1), F32)
    for c in range(columns // chunk):
        part = slice(c * chunk, (c + 1) * chunk)
        key = acc_k[:, part]
        key_squares += jnp.sum(key * key, axis=1, keepdims=True)
        scaled = hidden[:, part].astype(F32) * hg_ref[part].reshape(1, chunk) * (key * kg_ref[part].reshape(1, chunk))
        crossing += jnp.sum(scaled, axis=1, keepdims=True)
    lanes = lax.broadcasted_iota(jnp.int32, (requests, 128), 1)
    packed = jnp.where(lanes == 0, hidden_squares, jnp.where(lanes == 1, key_squares,
                       jnp.where(lanes == 2, crossing, 0.0)))
    stats[0] = packed.T[:8]

    def stat_copy(m):
        return there(stats.at[0], stats.at[m], stat_send.at[m - 1], stat_recv.at[m - 1], me_p, me_t ^ m)

    for m in range(1, heads):
        stat_copy(m).start()
    for m in range(1, heads):
        stat_copy(m).wait_recv()
    summed = stats[0]
    for m in range(1, heads):
        summed += stats[m]
    turned = jnp.concatenate([summed, jnp.zeros((120, requests), F32)], axis=0).T
    hidden_total, key_total, cross_total = turned[:, 0:1], turned[:, 1:2], turned[:, 2:3]
    agreement = (cross_total * lax.rsqrt(hidden_total / model + epsilon)
                 * lax.rsqrt(key_total / model + epsilon))
    gate = jax.nn.sigmoid(agreement / math.sqrt(model))
    for c in range(columns // chunk):
        part = slice(c * chunk, (c + 1) * chunk)
        out_ref[:, part] = (hidden[:, part].astype(F32) + gate * acc_v[:, part]).astype(BF16)

    for m in range(1, heads):
        id_copy(m, me_t).wait_send()
        stat_copy(m).wait_send()

    @pl.loop(1, groups)
    def _(i):
        list_copy(i, me_p).wait_send()
        for h in range(heads):
            row_copy(h, i, me_p).wait_send()

    for h in range(heads):
        masks = [0]
        for b in bits:
            for m in masks:
                pass_on(h, b, m, me_t ^ m).wait_send()
            masks = masks + [m | b for m in masks]


def local(groups, heads, hidden, hash_rows, memory_table, key_weight, value_weight, hidden_gain, key_gain):
    requests, columns = hidden.shape
    held, width = memory_table.shape
    assert hash_rows.shape[1] == 1 and heads & (heads - 1) == 0 and heads > 1
    slots = max(8, 2 * max(1, hash_rows.size // (groups * heads)))
    any_space = pl.BlockSpec(memory_space=pl.ANY)
    vmem = pl.BlockSpec(memory_space=pltpu.VMEM)
    dma = pltpu.SemaphoreType.DMA
    return pl.pallas_call(
        functools.partial(kernel, groups, heads, slots),
        out_shape=jax.ShapeDtypeStruct((requests, columns), BF16),
        in_specs=[vmem] * 3 + [any_space] * 4,
        out_specs=vmem,
        scratch_shapes=[
            pltpu.VMEM((groups, heads, 1, requests), jnp.int32),
            pltpu.VMEM((held, width), BF16),
            pltpu.VMEM((requests, columns), BF16),
            pltpu.VMEM((heads, width, columns), BF16),
            pltpu.VMEM((heads, width, columns), BF16),
            pltpu.VMEM((heads, groups, slots, width), BF16),
            pltpu.VMEM((heads, heads, groups, slots, width), BF16),
            pltpu.VMEM((heads, requests, groups * heads * slots), BF16),
            pltpu.VMEM((requests, width), BF16),
            pltpu.VMEM((requests, columns), F32),
            pltpu.VMEM((requests, columns), F32),
            pltpu.VMEM((heads, 8, requests), F32),
            dma((3,)), dma((heads, 2)), dma((heads,)),
            dma((heads - 1,)), dma((heads - 1,)),
            dma((groups - 1,)), dma((groups - 1,)),
            dma((heads, groups - 1)), dma((heads, groups - 1)),
            dma((heads, heads - 1)), dma((heads, heads - 1)),
            dma((heads - 1,)), dma((heads - 1,)),
        ],
        compiler_params=pltpu.CompilerParams(
            collective_id=0, has_side_effects=True, vmem_limit_bytes=60 * 1024 * 1024),
    )(hash_rows.reshape(1, 1, requests), hidden_gain, key_gain,
      memory_table, hidden, key_weight, value_weight)


def solution(mesh):
    return jax.shard_map(
        functools.partial(local, mesh.shape["dp"], mesh.shape["tensor"]),
        mesh=mesh,
        in_specs=(
            P("dp", "tensor"),
            P("dp", "tensor"),
            P(("dp", "tensor"), None),
            P(None, "tensor"),
            P(None, "tensor"),
            P("tensor"),
            P("tensor"),
        ),
        out_specs=P("dp", "tensor"),
        check_vma=False,
    )
```

```python
import functools
import math

import jax
import jax.numpy as jnp
from jax import lax
from jax.experimental import pallas as pl
from jax.experimental.pallas import tpu as pltpu
from jax.sharding import PartitionSpec as P

MESH = pl.DeviceIdType.MESH
epsilon = 1e-06
F32, BF16 = jnp.float32, jnp.bfloat16


def dot(a, b):
    return jnp.dot(a, b, preferred_element_type=F32)


def kernel(groups, heads, slots, ids_ref, hg_ref, kg_ref, table_hbm, hidden_hbm, wk_hbm, wv_hbm, out_ref,
           ids, table, hidden, wk, wv, sending, rows, place, mem, acc_k, acc_v, stats,
           local_sem, w_sem, own_sem, id_send, id_recv, list_send, list_recv,
           row_send, row_recv, pass_send, pass_recv, stat_send, stat_recv):
    me_p, me_t = lax.axis_index("dp"), lax.axis_index("tensor")
    held, width = table.shape
    requests, columns = hidden.shape
    model = columns * heads
    chunk = 256 if columns % 256 == 0 else 128

    def here(source, target, sem):
        return pltpu.make_async_copy(source, target, sem)

    def there(source, target, send, recv, p, t):
        return pltpu.make_async_remote_copy(
            src_ref=source, dst_ref=target, send_sem=send, recv_sem=recv,
            device_id={"dp": p, "tensor": t}, device_id_type=MESH)

    def ahead(i):
        return lax.rem(me_p + i, groups)

    def behind(i):
        return lax.rem(me_p + groups - i, groups)

    own_ids = here(ids_ref.at[0], ids.at[me_p, me_t], local_sem.at[0])
    own_ids.start()
    table_copy = here(table_hbm, table, local_sem.at[1])
    table_copy.start()
    weights = []
    for h in range(heads):
        for which, (source, target) in enumerate(((wk_hbm, wk), (wv_hbm, wv))):
            copy = here(source.at[pl.ds(h * width, width), :], target.at[h], w_sem.at[h, which])
            copy.start()
            weights.append(copy)
    hidden_copy = here(hidden_hbm, hidden, local_sem.at[2])
    hidden_copy.start()

    barrier = pltpu.get_barrier_semaphore()

    @pl.loop(1, groups)
    def _(i):
        pl.semaphore_signal(barrier, inc=1, device_id={"dp": ahead(i), "tensor": me_t}, device_id_type=MESH)

    for m in range(1, heads):
        pl.semaphore_signal(barrier, inc=1, device_id={"dp": me_p, "tensor": me_t ^ m}, device_id_type=MESH)
    pl.semaphore_wait(barrier, groups - 1 + heads - 1)

    def id_copy(m, t):
        return there(ids_ref.at[0], ids.at[me_p, t], id_send.at[m - 1], id_recv.at[m - 1], me_p, me_t ^ m)

    for m in range(1, heads):
        id_copy(m, me_t).start()
    own_ids.wait()
    for m in range(1, heads):
        id_copy(m, me_t ^ m).wait_recv()

    def list_copy(i, p):
        return there(ids.at[me_p], ids.at[p], list_send.at[i - 1], list_recv.at[i - 1], ahead(i), me_t)

    @pl.loop(1, groups)
    def _(i):
        list_copy(i, me_p).start()

    sub = lax.broadcasted_iota(jnp.int32, (requests, requests), 0)
    lane = lax.broadcasted_iota(jnp.int32, (requests, requests), 1)
    spots = lax.broadcasted_iota(jnp.int32, (requests, groups * heads * slots), 1).astype(F32)
    for h in range(heads):
        numbers = ids[me_p, h].astype(F32)
        owner = jnp.broadcast_to(jnp.floor((numbers + 0.5) * (1.0 / held)), (requests, requests))
        column = jnp.sum(jnp.where(sub == lane, owner, 0.0), axis=1, keepdims=True)
        rank = jnp.sum(jnp.where((owner == column) & (lane < sub), 1.0, 0.0), axis=1, keepdims=True)
        owner_p = jnp.floor((column + 0.5) * (1.0 / heads))
        owner_t = column - owner_p * heads
        spot = (owner_t * groups + owner_p) * slots + rank
        place[h] = jnp.where(spots == spot, 1.0, 0.0).astype(BF16)

    hidden_copy.wait()
    hidden_squares = jnp.zeros((requests, 1), F32)
    for c in range(columns // chunk):
        part = hidden[:, c * chunk:(c + 1) * chunk].astype(F32)
        hidden_squares += jnp.sum(part * part, axis=1, keepdims=True)

    @pl.loop(1, groups)
    def _(i):
        list_copy(i, behind(i)).wait_recv()

    lists = jnp.concatenate([ids[:, h].reshape(groups, requests) for h in range(heads)], axis=0)
    first = (me_p * heads + me_t) * held
    mine = (lists >= first) & (lists < first + held)
    earlier = jnp.where(sub < lane, 1.0, 0.0).astype(BF16)
    order = dot(jnp.where(mine, 1.0, 0.0).astype(BF16), earlier)
    order = jnp.where(mine, order, -1.0).astype(BF16)
    local = jnp.where(mine, lists - first, 0).astype(F32).astype(BF16)
    total = heads * groups * slots
    row = lax.broadcasted_iota(jnp.int32, (total, heads * groups), 0)
    source = lax.broadcasted_iota(jnp.int32, (total, heads * groups), 1) * slots
    spread = jnp.where((row >= source) & (row < source + slots), 1.0, 0.0).astype(BF16)
    slot = (lax.broadcasted_iota(jnp.int32, (total, requests), 0) & (slots - 1)).astype(F32)
    wanted = jnp.sum(jnp.where(dot(spread, order) == slot, dot(spread, local), 0.0), axis=1, keepdims=True)
    choose = jnp.where(
        lax.broadcasted_iota(jnp.int32, (total, held), 1).astype(F32) == wanted, 1.0, 0.0).astype(BF16)
    table_copy.wait()

    def row_copy(h, i, p):
        return there(sending.at[h, ahead(i)], rows.at[h, me_t, p],
                     row_send.at[h, i - 1], row_recv.at[h, i - 1], ahead(i), me_t)

    def send_rows(h):
        @pl.loop(1, groups)
        def _(i):
            row_copy(h, i, me_p).start()

    per_head = groups * slots
    for h in range(heads):
        block = dot(choose[h * per_head:(h + 1) * per_head], table[...])
        sending[h] = block.reshape(groups, slots, width).astype(BF16)
        here(sending.at[h, me_p], rows.at[h, me_t, me_p], own_sem.at[h]).start()
        if h < 2:
            send_rows(h)

    def pass_on(h, bit, m, t):
        return there(rows.at[h, me_t ^ m], rows.at[h, t], pass_send.at[h, (m | bit) - 1],
                     pass_recv.at[h, (m | bit) - 1], me_p, me_t ^ bit)

    bits, bit = [], heads // 2
    while bit:
        bits.append(bit)
        bit //= 2

    def begin(h):
        here(sending.at[h, me_p], rows.at[h, me_t, me_p], own_sem.at[h]).wait()

        @pl.loop(1, groups)
        def _(i):
            row_copy(h, i, behind(i)).wait_recv()

        for b in bits:
            pass_on(h, b, 0, me_t).start()
        if h + 2 < heads:
            send_rows(h + 2)

    def onward(h):
        masks = [0]
        for n, b in enumerate(bits):
            if n:
                for m in masks[1:]:
                    pass_on(h, b, m, me_t ^ m).start()
            if n < len(bits) - 1:
                for m in masks:
                    pass_on(h, b, m, me_t ^ m ^ b).wait_recv()
            masks = masks + [m | b for m in masks]

    def finish(h):
        b = bits[-1]
        for m in range(0, heads, 2):
            pass_on(h, b, m, me_t ^ m ^ b).wait_recv()

    def multiply(h):
        finish(h)
        mem[...] = dot(place[h], rows[h].reshape(groups * heads * slots, width)).astype(BF16)
        weights[2 * h].wait()
        weights[2 * h + 1].wait()

        for c in range(columns // chunk):
            part = pl.ds(c * chunk, chunk)
            for w, acc in ((wk, acc_k), (wv, acc_v)):
                value = dot(mem[...], w[h, :, part])
                acc[:, part] = value if h == 0 else acc[:, part] + value

    for step in range(heads + 2):
        if step < heads:
            begin(step)
        if step > 1:
            multiply(step - 2)
        if 0 < step <= heads:
            onward(step - 1)

    key_squares = jnp.zeros((requests, 1), F32)
    crossing = jnp.zeros((requests, 1), F32)
    for c in range(columns // chunk):
        part = slice(c * chunk, (c + 1) * chunk)
        key = acc_k[:, part]
        key_squares += jnp.sum(key * key, axis=1, keepdims=True)
        scaled = hidden[:, part].astype(F32) * hg_ref[part].reshape(1, chunk) * (key * kg_ref[part].reshape(1, chunk))
        crossing += jnp.sum(scaled, axis=1, keepdims=True)
    lanes = lax.broadcasted_iota(jnp.int32, (requests, 128), 1)
    packed = jnp.where(lanes == 0, hidden_squares, jnp.where(lanes == 1, key_squares,
                       jnp.where(lanes == 2, crossing, 0.0)))
    stats[0] = packed.T[:8]

    def stat_copy(m):
        return there(stats.at[0], stats.at[m], stat_send.at[m - 1], stat_recv.at[m - 1], me_p, me_t ^ m)

    for m in range(1, heads):
        stat_copy(m).start()
    for m in range(1, heads):
        stat_copy(m).wait_recv()
    summed = stats[0]
    for m in range(1, heads):
        summed += stats[m]
    turned = jnp.concatenate([summed, jnp.zeros((120, requests), F32)], axis=0).T
    hidden_total, key_total, cross_total = turned[:, 0:1], turned[:, 1:2], turned[:, 2:3]
    agreement = (cross_total * lax.rsqrt(hidden_total / model + epsilon)
                 * lax.rsqrt(key_total / model + epsilon))
    gate = jax.nn.sigmoid(agreement / math.sqrt(model))
    for c in range(columns // chunk):
        part = slice(c * chunk, (c + 1) * chunk)
        out_ref[:, part] = (hidden[:, part].astype(F32) + gate * acc_v[:, part]).astype(BF16)

    for m in range(1, heads):
        id_copy(m, me_t).wait_send()
        stat_copy(m).wait_send()

    @pl.loop(1, groups)
    def _(i):
        list_copy(i, me_p).wait_send()
        for h in range(heads):
            row_copy(h, i, me_p).wait_send()

    for h in range(heads):
        masks = [0]
        for b in bits:
            for m in masks:
                pass_on(h, b, m, me_t ^ m).wait_send()
            masks = masks + [m | b for m in masks]


def local(groups, heads, hidden, hash_rows, memory_table, key_weight, value_weight, hidden_gain, key_gain):
    requests, columns = hidden.shape
    held, width = memory_table.shape
    assert hash_rows.shape[1] == 1 and heads & (heads - 1) == 0 and heads > 1
    slots = max(8, 2 * max(1, hash_rows.size // (groups * heads)))
    any_space = pl.BlockSpec(memory_space=pl.ANY)
    vmem = pl.BlockSpec(memory_space=pltpu.VMEM)
    dma = pltpu.SemaphoreType.DMA
    return pl.pallas_call(
        functools.partial(kernel, groups, heads, slots),
        out_shape=jax.ShapeDtypeStruct((requests, columns), BF16),
        in_specs=[vmem] * 3 + [any_space] * 4,
        out_specs=vmem,
        scratch_shapes=[
            pltpu.VMEM((groups, heads, 1, requests), jnp.int32),
            pltpu.VMEM((held, width), BF16),
            pltpu.VMEM((requests, columns), BF16),
            pltpu.VMEM((heads, width, columns), BF16),
            pltpu.VMEM((heads, width, columns), BF16),
            pltpu.VMEM((heads, groups, slots, width), BF16),
            pltpu.VMEM((heads, heads, groups, slots, width), BF16),
            pltpu.VMEM((heads, requests, groups * heads * slots), BF16),
            pltpu.VMEM((requests, width), BF16),
            pltpu.VMEM((requests, columns), F32),
            pltpu.VMEM((requests, columns), F32),
            pltpu.VMEM((heads, 8, requests), F32),
            dma((3,)), dma((heads, 2)), dma((heads,)),
            dma((heads - 1,)), dma((heads - 1,)),
            dma((groups - 1,)), dma((groups - 1,)),
            dma((heads, groups - 1)), dma((heads, groups - 1)),
            dma((heads, heads - 1)), dma((heads, heads - 1)),
            dma((heads - 1,)), dma((heads - 1,)),
        ],
        compiler_params=pltpu.CompilerParams(
            collective_id=0, has_side_effects=True, vmem_limit_bytes=60 * 1024 * 1024),
    )(hash_rows.reshape(1, 1, requests), hidden_gain, key_gain,
      memory_table, hidden, key_weight, value_weight)


def solution(mesh):
    return jax.shard_map(
        functools.partial(local, mesh.shape["dp"], mesh.shape["tensor"]),
        mesh=mesh,
        in_specs=(
            P("dp", "tensor"),
            P("dp", "tensor"),
            P(("dp", "tensor"), None),
            P(None, "tensor"),
            P(None, "tensor"),
            P("tensor"),
            P("tensor"),
        ),
        out_specs=P("dp", "tensor"),
        check_vma=False,
    )
```

```python
import functools
import math

import jax
import jax.numpy as jnp
from jax import lax
from jax.experimental import pallas as pl
from jax.experimental.pallas import tpu as pltpu
from jax.sharding import PartitionSpec as P

MESH = pl.DeviceIdType.MESH
epsilon = 1e-06
F32, BF16 = jnp.float32, jnp.bfloat16


def dot(a, b):
    return jnp.dot(a, b, preferred_element_type=F32)


def kernel(groups, heads, slots, ids_ref, hg_ref, kg_ref, table_hbm, hidden_hbm, wk_hbm, wv_hbm, out_ref,
           ids, table, hidden, wk, wv, sending, rows, place, mem, acc_k, acc_v, stats,
           local_sem, w_sem, own_sem, id_send, id_recv, list_send, list_recv,
           row_send, row_recv, pass_send, pass_recv, stat_send, stat_recv):
    me_p, me_t = lax.axis_index("dp"), lax.axis_index("tensor")
    held, width = table.shape
    requests, columns = hidden.shape
    model = columns * heads
    chunk = 256 if columns % 256 == 0 else 128

    def here(source, target, sem):
        return pltpu.make_async_copy(source, target, sem)

    def there(source, target, send, recv, p, t):
        return pltpu.make_async_remote_copy(
            src_ref=source, dst_ref=target, send_sem=send, recv_sem=recv,
            device_id={"dp": p, "tensor": t}, device_id_type=MESH)

    def ahead(i):
        return lax.rem(me_p + i, groups)

    def behind(i):
        return lax.rem(me_p + groups - i, groups)

    own_ids = here(ids_ref.at[0], ids.at[me_p, me_t], local_sem.at[0])
    own_ids.start()
    table_copy = here(table_hbm, table, local_sem.at[1])
    table_copy.start()
    weights = []
    for h in range(heads):
        for which, (source, target) in enumerate(((wk_hbm, wk), (wv_hbm, wv))):
            copy = here(source.at[pl.ds(h * width, width), :], target.at[h], w_sem.at[h, which])
            copy.start()
            weights.append(copy)
    hidden_copy = here(hidden_hbm, hidden, local_sem.at[2])
    hidden_copy.start()

    barrier = pltpu.get_barrier_semaphore()

    @pl.loop(1, groups)
    def _(i):
        pl.semaphore_signal(barrier, inc=1, device_id={"dp": ahead(i), "tensor": me_t}, device_id_type=MESH)

    for m in range(1, heads):
        pl.semaphore_signal(barrier, inc=1, device_id={"dp": me_p, "tensor": me_t ^ m}, device_id_type=MESH)
    pl.semaphore_wait(barrier, groups - 1 + heads - 1)

    def id_copy(m, t):
        return there(ids_ref.at[0], ids.at[me_p, t], id_send.at[m - 1], id_recv.at[m - 1], me_p, me_t ^ m)

    for m in range(1, heads):
        id_copy(m, me_t).start()
    own_ids.wait()
    for m in range(1, heads):
        id_copy(m, me_t ^ m).wait_recv()

    def list_copy(i, p):
        return there(ids.at[me_p], ids.at[p], list_send.at[i - 1], list_recv.at[i - 1], ahead(i), me_t)

    @pl.loop(1, groups)
    def _(i):
        list_copy(i, me_p).start()

    sub = lax.broadcasted_iota(jnp.int32, (requests, requests), 0)
    lane = lax.broadcasted_iota(jnp.int32, (requests, requests), 1)
    spots = lax.broadcasted_iota(jnp.int32, (requests, groups * heads * slots), 1).astype(F32)
    for h in range(heads):
        numbers = ids[me_p, h].astype(F32)
        owner = jnp.broadcast_to(jnp.floor((numbers + 0.5) * (1.0 / held)), (requests, requests))
        column = jnp.sum(jnp.where(sub == lane, owner, 0.0), axis=1, keepdims=True)
        rank = jnp.sum(jnp.where((owner == column) & (lane < sub), 1.0, 0.0), axis=1, keepdims=True)
        owner_p = jnp.floor((column + 0.5) * (1.0 / heads))
        owner_t = column - owner_p * heads
        spot = (owner_t * groups + owner_p) * slots + rank
        place[h] = jnp.where(spots == spot, 1.0, 0.0).astype(BF16)

    hidden_copy.wait()
    hidden_squares = jnp.zeros((requests, 1), F32)
    for c in range(columns // chunk):
        part = hidden[:, c * chunk:(c + 1) * chunk].astype(F32)
        hidden_squares += jnp.sum(part * part, axis=1, keepdims=True)

    @pl.loop(1, groups)
    def _(i):
        list_copy(i, behind(i)).wait_recv()

    lists = jnp.concatenate([ids[:, h].reshape(groups, requests) for h in range(heads)], axis=0)
    first = (me_p * heads + me_t) * held
    mine = (lists >= first) & (lists < first + held)
    earlier = jnp.where(sub < lane, 1.0, 0.0).astype(BF16)
    order = dot(jnp.where(mine, 1.0, 0.0).astype(BF16), earlier)
    order = jnp.where(mine, order, -1.0).astype(BF16)
    local = jnp.where(mine, lists - first, 0).astype(F32).astype(BF16)
    total = heads * groups * slots
    row = lax.broadcasted_iota(jnp.int32, (total, heads * groups), 0)
    source = lax.broadcasted_iota(jnp.int32, (total, heads * groups), 1) * slots
    spread = jnp.where((row >= source) & (row < source + slots), 1.0, 0.0).astype(BF16)
    slot = (lax.broadcasted_iota(jnp.int32, (total, requests), 0) & (slots - 1)).astype(F32)
    wanted = jnp.sum(jnp.where(dot(spread, order) == slot, dot(spread, local), 0.0), axis=1, keepdims=True)
    choose = jnp.where(
        lax.broadcasted_iota(jnp.int32, (total, held), 1).astype(F32) == wanted, 1.0, 0.0).astype(BF16)
    table_copy.wait()

    def row_copy(h, i, p):
        return there(sending.at[h, ahead(i)], rows.at[h, me_t, p],
                     row_send.at[h, i - 1], row_recv.at[h, i - 1], ahead(i), me_t)

    def send_rows(h):
        @pl.loop(1, groups)
        def _(i):
            row_copy(h, i, me_p).start()

    per_head = groups * slots
    for h in range(heads):
        block = dot(choose[h * per_head:(h + 1) * per_head], table[...])
        sending[h] = block.reshape(groups, slots, width).astype(BF16)
        here(sending.at[h, me_p], rows.at[h, me_t, me_p], own_sem.at[h]).start()
        if h < 3:
            send_rows(h)

    def pass_on(h, bit, m, t):
        return there(rows.at[h, me_t ^ m], rows.at[h, t], pass_send.at[h, (m | bit) - 1],
                     pass_recv.at[h, (m | bit) - 1], me_p, me_t ^ bit)

    bits, bit = [], heads // 2
    while bit:
        bits.append(bit)
        bit //= 2

    def begin(h):
        here(sending.at[h, me_p], rows.at[h, me_t, me_p], own_sem.at[h]).wait()

        @pl.loop(1, groups)
        def _(i):
            row_copy(h, i, behind(i)).wait_recv()

        for b in bits:
            pass_on(h, b, 0, me_t).start()
        if h + 3 < heads:
            send_rows(h + 3)

    def onward(h):
        masks = [0]
        for n, b in enumerate(bits):
            if n:
                for m in masks[1:]:
                    pass_on(h, b, m, me_t ^ m).start()
            if n < len(bits) - 1:
                for m in masks:
                    pass_on(h, b, m, me_t ^ m ^ b).wait_recv()
            masks = masks + [m | b for m in masks]

    def finish(h):
        b = bits[-1]
        for m in range(0, heads, 2):
            pass_on(h, b, m, me_t ^ m ^ b).wait_recv()

    def multiply(h):
        finish(h)
        mem[...] = dot(place[h], rows[h].reshape(groups * heads * slots, width)).astype(BF16)
        weights[2 * h].wait()
        weights[2 * h + 1].wait()

        for c in range(columns // chunk):
            part = pl.ds(c * chunk, chunk)
            for w, acc in ((wk, acc_k), (wv, acc_v)):
                value = dot(mem[...], w[h, :, part])
                acc[:, part] = value if h == 0 else acc[:, part] + value

    for step in range(heads + 2):
        if step < heads:
            begin(step)
        if step > 1:
            multiply(step - 2)
        if 0 < step <= heads:
            onward(step - 1)

    key_squares = jnp.zeros((requests, 1), F32)
    crossing = jnp.zeros((requests, 1), F32)
    for c in range(columns // chunk):
        part = slice(c * chunk, (c + 1) * chunk)
        key = acc_k[:, part]
        key_squares += jnp.sum(key * key, axis=1, keepdims=True)
        scaled = hidden[:, part].astype(F32) * hg_ref[part].reshape(1, chunk) * (key * kg_ref[part].reshape(1, chunk))
        crossing += jnp.sum(scaled, axis=1, keepdims=True)
    lanes = lax.broadcasted_iota(jnp.int32, (requests, 128), 1)
    packed = jnp.where(lanes == 0, hidden_squares, jnp.where(lanes == 1, key_squares,
                       jnp.where(lanes == 2, crossing, 0.0)))
    stats[0] = packed.T[:8]

    def stat_copy(m):
        return there(stats.at[0], stats.at[m], stat_send.at[m - 1], stat_recv.at[m - 1], me_p, me_t ^ m)

    for m in range(1, heads):
        stat_copy(m).start()
    for m in range(1, heads):
        stat_copy(m).wait_recv()
    summed = stats[0]
    for m in range(1, heads):
        summed += stats[m]
    turned = jnp.concatenate([summed, jnp.zeros((120, requests), F32)], axis=0).T
    hidden_total, key_total, cross_total = turned[:, 0:1], turned[:, 1:2], turned[:, 2:3]
    agreement = (cross_total * lax.rsqrt(hidden_total / model + epsilon)
                 * lax.rsqrt(key_total / model + epsilon))
    gate = jax.nn.sigmoid(agreement / math.sqrt(model))
    for c in range(columns // chunk):
        part = slice(c * chunk, (c + 1) * chunk)
        out_ref[:, part] = (hidden[:, part].astype(F32) + gate * acc_v[:, part]).astype(BF16)

    for m in range(1, heads):
        id_copy(m, me_t).wait_send()
        stat_copy(m).wait_send()

    @pl.loop(1, groups)
    def _(i):
        list_copy(i, me_p).wait_send()
        for h in range(heads):
            row_copy(h, i, me_p).wait_send()

    for h in range(heads):
        masks = [0]
        for b in bits:
            for m in masks:
                pass_on(h, b, m, me_t ^ m).wait_send()
            masks = masks + [m | b for m in masks]


def local(groups, heads, hidden, hash_rows, memory_table, key_weight, value_weight, hidden_gain, key_gain):
    requests, columns = hidden.shape
    held, width = memory_table.shape
    assert hash_rows.shape[1] == 1 and heads & (heads - 1) == 0 and heads > 1
    slots = max(8, 2 * max(1, hash_rows.size // (groups * heads)))
    any_space = pl.BlockSpec(memory_space=pl.ANY)
    vmem = pl.BlockSpec(memory_space=pltpu.VMEM)
    dma = pltpu.SemaphoreType.DMA
    return pl.pallas_call(
        functools.partial(kernel, groups, heads, slots),
        out_shape=jax.ShapeDtypeStruct((requests, columns), BF16),
        in_specs=[vmem] * 3 + [any_space] * 4,
        out_specs=vmem,
        scratch_shapes=[
            pltpu.VMEM((groups, heads, 1, requests), jnp.int32),
            pltpu.VMEM((held, width), BF16),
            pltpu.VMEM((requests, columns), BF16),
            pltpu.VMEM((heads, width, columns), BF16),
            pltpu.VMEM((heads, width, columns), BF16),
            pltpu.VMEM((heads, groups, slots, width), BF16),
            pltpu.VMEM((heads, heads, groups, slots, width), BF16),
            pltpu.VMEM((heads, requests, groups * heads * slots), BF16),
            pltpu.VMEM((requests, width), BF16),
            pltpu.VMEM((requests, columns), F32),
            pltpu.VMEM((requests, columns), F32),
            pltpu.VMEM((heads, 8, requests), F32),
            dma((3,)), dma((heads, 2)), dma((heads,)),
            dma((heads - 1,)), dma((heads - 1,)),
            dma((groups - 1,)), dma((groups - 1,)),
            dma((heads, groups - 1)), dma((heads, groups - 1)),
            dma((heads, heads - 1)), dma((heads, heads - 1)),
            dma((heads - 1,)), dma((heads - 1,)),
        ],
        compiler_params=pltpu.CompilerParams(
            collective_id=0, has_side_effects=True, vmem_limit_bytes=60 * 1024 * 1024),
    )(hash_rows.reshape(1, 1, requests), hidden_gain, key_gain,
      memory_table, hidden, key_weight, value_weight)


def solution(mesh):
    return jax.shard_map(
        functools.partial(local, mesh.shape["dp"], mesh.shape["tensor"]),
        mesh=mesh,
        in_specs=(
            P("dp", "tensor"),
            P("dp", "tensor"),
            P(("dp", "tensor"), None),
            P(None, "tensor"),
            P(None, "tensor"),
            P("tensor"),
            P("tensor"),
        ),
        out_specs=P("dp", "tensor"),
        check_vma=False,
    )
```
